32 devices in a mesh: row: 4 (over x, core), col: 8 (over z, y).
Axes of the slice: x: 2, y: 2, z: 4, core: 2. Of those that a mesh axis runs over, the one named last changes fastest.
Arguments:
- front: bfloat16 [24576, 24576], P('row', 'col'), may hold values from -6 to 6
- diag_inverse: bfloat16 [256, 256], replicated, as said below
- fill_pattern: int32 [384, 384], replicated, may hold values from 0 to 1, as said below
Outputs:
- updated: bfloat16 [24576, 24576], P('row', 'col')
The draws below stay inside these ranges and needn't reach their ends.
Inputs may be any that keep to these rules, and one draw needn't show every extreme that they name: `fill_pattern`: symmetric, with ones on the diagonal. `diag_inverse`: lower triangular.
All inputs are finite; a program needn't handle non-finite values.
Results may differ from the reference program's by a relative error of at most 0.0045.
Values may be sent and summed in bfloat16 or wider, within the bound.
A program may use at most 128 MiB of HBM per device.

```python
import jax
import jax.numpy as jnp
from jax import lax

M = 24576
B = 64
P_SIZE = 256
N_ROW = 4
N_COL = 8


def draw_fill_pattern(key, part):
    count = M // B
    values = jax.random.randint(key, (count, count), 0, 4)
    marks = (values < 3).astype(jnp.int32)
    both = marks * marks.T
    ident = jnp.eye(count, dtype=jnp.int32)
    return jnp.maximum(both, ident)


def draw_diag_inverse(key, part):
    first = jax.random.fold_in(key, 0)
    values = jax.random.normal(first, (P_SIZE, P_SIZE), jnp.float32)
    scales = jnp.ones((P_SIZE, 1), jnp.float32)
    index = jnp.arange(P_SIZE, dtype=jnp.int32)
    lower = (index[:, None] >= index[None, :]).astype(jnp.float32)
    counts = (index + 1).astype(jnp.float32)[:, None]
    weights = 0.25 * scales * values * lower / jnp.sqrt(counts)
    weights = weights + 0.2 * jnp.eye(P_SIZE, dtype=jnp.float32)
    return weights.astype(jnp.bfloat16)


def block_levels(stream_key, shape, shards, least, high):
    def one(position, parts):
        heights = jax.random.uniform(jax.random.fold_in(jax.random.fold_in(stream_key, 6), position), (parts,), jnp.float32, least / len(shards), high / len(shards))
        return jnp.repeat(jnp.exp(heights), shape[position] // parts).reshape((-1,) + (1,) * (len(shape) - position - 1))

    loudness = one(*shards[0])
    for cut in shards[1:]:
        loudness = loudness * one(*cut)
    return loudness


def bell_draw(key, shape, scale, limit, cuts=(), held_as=jnp.bfloat16):
    loudness = block_levels(key, shape, cuts, -0.22, 0.18) if cuts else 1.0
    result = jax.random.normal(key, shape, jnp.float32) * scale * loudness
    return jnp.minimum(jnp.maximum(result, -limit), limit).astype(held_as)


def setup_inputs(seed: int = 0) -> dict:
    streams_of = jax.random.split(jax.random.key(seed), 4)
    front = bell_draw(streams_of[0], (M, M), 1.0, 6.0, ((0, 4), (1, 8)))
    diag_inverse = draw_diag_inverse(jax.random.fold_in(streams_of[3], 71), 0)
    fill_pattern = draw_fill_pattern(jax.random.fold_in(streams_of[3], 71), 0)
    return dict(front=front, diag_inverse=diag_inverse, fill_pattern=fill_pattern)


def reference(front, diag_inverse, fill_pattern):
    blocks = M // B
    local_rows = M // (B * N_ROW)
    local_cols = M // (B * N_COL)
    panel_blocks = P_SIZE // B
    stored = jnp.arange(blocks, dtype=jnp.int32)
    row_global = (stored % local_rows) * N_ROW + stored // local_rows
    col_global = (stored % local_cols) * N_COL + stored // local_cols
    panel = jnp.concatenate([front[:, h * local_cols * B:h * local_cols * B + B] for h in range(panel_blocks)], axis=1)
    factor = jnp.dot(panel, diag_inverse.T, preferred_element_type=jnp.float32).astype(jnp.bfloat16)
    source = (col_global % N_ROW) * local_rows + col_global // N_ROW
    col_factor = factor.reshape(blocks, B, P_SIZE)[source].reshape(M, P_SIZE)
    keep = fill_pattern[row_global][:, col_global].astype(jnp.float32)
    keep = keep * (row_global >= panel_blocks).astype(jnp.float32)[:, None]
    keep = keep * (col_global >= panel_blocks).astype(jnp.float32)[None, :]

    def one_block(items):
        front_rows, factor_rows, keep_row = items
        product = jnp.dot(factor_rows, col_factor.T, preferred_element_type=jnp.float32)
        spread = jnp.repeat(keep_row, B)
        return (front_rows.astype(jnp.float32) - product * spread[None, :]).astype(jnp.bfloat16)

    updated = lax.map(one_block, (front.reshape(blocks, B, M), factor.reshape(blocks, B, P_SIZE), keep))
    updated = updated.reshape(M, M)
    for h in range(panel_blocks):
        updated = updated.at[:, h * local_cols * B:h * local_cols * B + B].set(factor[:, h * B:(h + 1) * B])
    return updated
```

```python
import functools

import jax
import jax.numpy as jnp
from jax import lax
from jax.experimental import pallas as pl
from jax.experimental.pallas import tpu as pltpu
from jax.sharding import PartitionSpec as P

B = 64
P_SIZE = 256
LANES = 128
AHEAD = 3
MESH = pl.DeviceIdType.MESH
NT = (((1,), (1,)), ((), ()))


def nt_dot(a, b):
    return lax.dot_general(a, b, NT, preferred_element_type=jnp.float32)


def nn_dot(a, b):
    return jnp.dot(a, b, preferred_element_type=jnp.float32)


def one_hot(shape, test):
    i = lax.broadcasted_iota(jnp.int32, shape, 0)
    j = lax.broadcasted_iota(jnp.int32, shape, 1)
    return jnp.where(test(i, j), 1.0, 0.0).astype(jnp.bfloat16)


def gather_kernel(
    n_row, n_col,
    front, diag, fill, out,
    source, pan, colp, fac, colf, keep, w_lo, w_hi,
    load_sem, source_sem, row_recv, row_send, col_recv, col_send,
):
    r = lax.axis_index("row")
    c = lax.axis_index("col")
    rows, cols = out.shape
    heads = P_SIZE // B
    ratio = n_col // n_row
    half = 2 * ratio * B
    step_rows = 2 * half
    step_cols = step_rows // ratio
    chunks = rows // step_rows
    outer, inner = 4, n_col // 4
    a = c // inner
    b = c % inner
    owner = c < heads
    x, core = r // 2, r % 2
    source_row = c % n_row
    source_x, source_core = source_row // 2, source_row % 2
    parity = c // n_row
    n_x = n_row // 2

    def load(k):
        part = pl.ds(pl.multiple_of(k * step_rows, step_rows), step_rows)
        return pltpu.make_async_copy(front.at[part], out.at[part], load_sem.at[k])

    def fetch():
        return pltpu.make_async_copy(front.at[:, 0:LANES], source, source_sem)

    def row_copy(k, h, slot, target):
        return pltpu.make_async_remote_copy(
            src_ref=pan.at[k, h], dst_ref=pan.at[k, h],
            send_sem=row_send.at[k, h, slot], recv_sem=row_recv.at[k, h],
            device_id=(r, target), device_id_type=MESH,
        )

    def row_sends(k, h, act):
        a_h, b_h = h // inner, h % inner

        @pl.when(b == b_h)
        def _():
            @pl.when(jnp.logical_and(a >= a_h, a < outer - 1))
            def _():
                act(row_copy(k, h, 0, c + inner))

            @pl.when(jnp.logical_and(a <= a_h, a > 0))
            def _():
                act(row_copy(k, h, 1, c - inner))

            for d in range(1, inner):
                act(row_copy(k, h, 1 + d, a * inner + (b + d) % inner))

    def col_copy(k, src, slot, target):
        return pltpu.make_async_remote_copy(
            src_ref=src, dst_ref=colp.at[k],
            send_sem=col_send.at[k, slot], recv_sem=col_recv.at[k],
            device_id=(target, c), device_id_type=MESH,
        )

    def col_local(k):
        return pltpu.make_async_copy(pan.at[k, :, :, parity], colp.at[k], col_recv.at[k])

    is_source = r == source_row
    is_relay = jnp.logical_and(core == source_core, x != source_x)

    def col_source_sends(k, act):
        @pl.when(is_source)
        def _():
            src = pan.at[k, :, :, parity]
            for d in range(1, n_x):
                act(col_copy(k, src, d, ((x + d) % n_x) * 2 + core))
            act(col_copy(k, src, 0, x * 2 + 1 - core))

    def col_relay_sends(k, act):
        @pl.when(is_relay)
        def _():
            act(col_copy(k, colp.at[k], 0, x * 2 + 1 - core))

    @pl.when(owner)
    def _():
        fetch().start()

    for k in range(chunks):
        load(k).start()

    barrier = pltpu.get_barrier_semaphore()

    @pl.when(a > 0)
    def _():
        pl.semaphore_signal(barrier, inc=1, device_id=(r, c - inner), device_id_type=MESH)

    @pl.when(a < outer - 1)
    def _():
        pl.semaphore_signal(barrier, inc=1, device_id=(r, c + inner), device_id_type=MESH)

    for d in range(1, inner):
        pl.semaphore_signal(
            barrier, inc=1, device_id=(r, a * inner + (b + d) % inner), device_id_type=MESH
        )
    for d in range(1, n_row):
        pl.semaphore_signal(barrier, inc=1, device_id=((r + d) % n_row, c), device_id_type=MESH)

    @pl.when(owner)
    def _():
        fetch().wait()
        to_lo = one_hot((LANES, LANES), lambda i, j: (i == j) & (i < B))
        to_hi = one_hot((LANES, LANES), lambda i, j: (i + B == j) & (i < B))

        def pack(k, _):
            at = pl.multiple_of(k * step_rows, step_rows)
            both = nn_dot(source[pl.ds(at, half), :], to_lo)
            both += nn_dot(source[pl.ds(at + half, half), :], to_hi)
            pan[k, c] = both.astype(jnp.bfloat16).reshape(2, ratio, B, LANES)
            return 0

        lax.fori_loop(0, chunks, pack, 0)

    extra = jnp.where(a > 0, 1, 0) + jnp.where(a < outer - 1, 1, 0)
    pl.semaphore_wait(barrier, inner - 1 + n_row - 1 + extra)

    def own_sends(k, act):
        for h in range(heads):
            @pl.when(c == h)
            def _():
                row_sends(k, h, act)

    for k in range(min(AHEAD, chunks)):
        own_sends(k, lambda copy: copy.start())

    def spread(shift):
        return one_hot(
            (P_SIZE, heads * LANES),
            lambda i, j: (i == (j // LANES) * B + j % LANES - shift)
            & (j % LANES >= shift) & (j % LANES < shift + B),
        )

    w_lo[...] = nn_dot(diag[...], spread(0)).astype(jnp.bfloat16)
    w_hi[...] = nn_dot(diag[...], spread(B)).astype(jnp.bfloat16)

    count = fill.shape[0]
    local_rows = rows // B
    pick = one_hot((local_rows, count), lambda i, j: j == i * n_row + r)
    picked = nn_dot(pick, fill[...].astype(jnp.float32).astype(jnp.bfloat16)).astype(jnp.bfloat16)

    def make_keep(j, _):
        at = pl.multiple_of(j * step_cols, step_cols)
        widen = one_hot(
            (count, step_cols), lambda i, l: i == ((at + l) // B) * n_col + c
        )
        wide = nn_dot(picked, widen)
        i = lax.broadcasted_iota(jnp.int32, wide.shape, 0)
        l = lax.broadcasted_iota(jnp.int32, wide.shape, 1)
        live = (i * n_row + r >= heads) & (((at + l) // B) * n_col + c >= heads)
        keep[:, pl.ds(at, step_cols)] = jnp.where(live, wide, 0.0)
        return 0

    lax.fori_loop(0, cols // step_cols, make_keep, 0)

    step_blocks = step_rows // B
    to_front = one_hot((P_SIZE, LANES), lambda i, l: (i == c * B + l) & (l < B))

    def tile(i, j):
        row_at = pl.multiple_of(i * step_rows, step_rows)
        col_at = pl.multiple_of(j * step_cols, step_cols)
        part = (pl.ds(row_at, step_rows), pl.ds(col_at, step_cols))
        product = nt_dot(fac[part[0], :], colf[part[1], :])
        marks = keep[pl.ds(pl.multiple_of(i * step_blocks, step_blocks), step_blocks), part[1]]
        masked = product.reshape(step_blocks, B, step_cols) * marks[:, None, :]
        value = out[part].astype(jnp.float32) - masked.reshape(step_rows, step_cols)
        out[part] = value.astype(jnp.bfloat16)

    def arrive(k):
        @pl.when(k + AHEAD < chunks)
        def _():
            own_sends(k + AHEAD, lambda copy: copy.start())

        for h in range(heads):
            @pl.when(c != h)
            def _():
                row_copy(k, h, 0, c).wait_recv()
                row_sends(k, h, lambda copy: copy.start())

        col_source_sends(k, lambda copy: copy.start())

        @pl.when(is_source)
        def _():
            col_local(k).start()

    def factors(k):
        packed = jnp.concatenate(
            [pan[k, h].reshape(half, LANES) for h in range(heads)], axis=1
        )
        at = pl.multiple_of(k * step_rows, step_rows)
        fac[pl.ds(at, half), :] = nt_dot(packed, w_lo[...]).astype(jnp.bfloat16)
        fac[pl.ds(at + half, half), :] = nt_dot(packed, w_hi[...]).astype(jnp.bfloat16)

    def col_factors(k):
        @pl.when(is_source)
        def _():
            col_local(k).wait()

        @pl.when(jnp.logical_not(is_source))
        def _():
            col_copy(k, colp.at[k], 0, r).wait_recv()

        col_relay_sends(k, lambda copy: copy.start())
        packed = jnp.concatenate(
            [colp[k, h].reshape(2 * B, LANES) for h in range(heads)], axis=1
        )
        at = pl.multiple_of(k * step_cols, step_cols)
        colf[pl.ds(at, 2 * B), :] = nt_dot(packed, w_lo[...]).astype(jnp.bfloat16)
        colf[pl.ds(at + 2 * B, 2 * B), :] = nt_dot(packed, w_hi[...]).astype(jnp.bfloat16)

    def wave(k):
        lax.fori_loop(0, k + 1, lambda j, _: (tile(k, j), 0)[1], 0)
        lax.fori_loop(0, k, lambda i, _: (tile(i, k), 0)[1], 0)

        @pl.when(owner)
        def _():
            at = pl.ds(pl.multiple_of(k * step_rows, step_rows), step_rows)
            piece = nn_dot(fac[at, :], to_front)
            old = out[at, 0:LANES].astype(jnp.float32)
            lane = lax.broadcasted_iota(jnp.int32, old.shape, 1)
            out[at, 0:LANES] = jnp.where(lane < B, piece, old).astype(jnp.bfloat16)

    def step(k, _):
        @pl.when(k < chunks)
        def _():
            arrive(k)
            factors(k)

        @pl.when(k > 0)
        def _():
            col_factors(k - 1)
            load(k - 1).wait()
            wave(k - 1)

        return 0

    lax.fori_loop(0, chunks + 1, step, 0)

    def drain(k, _):
        for h in range(heads):
            row_sends(k, h, lambda copy: copy.wait_send())
        col_source_sends(k, lambda copy: copy.wait_send())
        col_relay_sends(k, lambda copy: copy.wait_send())
        return 0

    lax.fori_loop(0, chunks, drain, 0)


def store_kernel(value, out, sems):
    parts = sems.shape[0]
    size = value.shape[0] // parts
    copies = [
        pltpu.make_async_copy(
            value.at[pl.ds(i * size, size)], out.at[pl.ds(i * size, size)], sems.at[i]
        )
        for i in range(parts)
    ]
    for copy in copies:
        copy.start()
    for copy in copies:
        copy.wait()


def body(front, diag_inverse, fill_pattern):
    rows, cols = front.shape
    n_row = lax.axis_size("row")
    n_col = lax.axis_size("col")
    heads = P_SIZE // B
    ratio = n_col // n_row
    step_rows = 4 * ratio * B
    chunks = rows // step_rows
    inner = n_col // 4
    bf16 = jnp.bfloat16
    any_space = pl.BlockSpec(memory_space=pl.ANY)
    vmem = pl.BlockSpec(memory_space=pltpu.VMEM)
    held = pl.pallas_call(
        functools.partial(gather_kernel, n_row, n_col),
        out_shape=pltpu.VMEM((rows, cols), bf16),
        in_specs=[any_space, vmem, vmem],
        out_specs=vmem,
        scratch_shapes=[
            pltpu.VMEM((rows, LANES), bf16),
            pltpu.VMEM((chunks, heads, 2, ratio, B, LANES), bf16),
            pltpu.VMEM((chunks, heads, 2, B, LANES), bf16),
            pltpu.VMEM((rows, P_SIZE), bf16),
            pltpu.VMEM((cols, P_SIZE), bf16),
            pltpu.VMEM((rows // B, cols), jnp.float32),
            pltpu.VMEM((P_SIZE, heads * LANES), bf16),
            pltpu.VMEM((P_SIZE, heads * LANES), bf16),
            pltpu.SemaphoreType.DMA((chunks,)),
            pltpu.SemaphoreType.DMA,
            pltpu.SemaphoreType.DMA((chunks, heads)),
            pltpu.SemaphoreType.DMA((chunks, heads, inner + 1)),
            pltpu.SemaphoreType.DMA((chunks,)),
            pltpu.SemaphoreType.DMA((chunks, n_row // 2)),
        ],
        compiler_params=pltpu.CompilerParams(
            collective_id=0, has_side_effects=True, vmem_limit_bytes=20 * 2**20
        ),
        name="gather_update",
    )(front, diag_inverse, fill_pattern)
    return pl.pallas_call(
        store_kernel,
        out_shape=jax.ShapeDtypeStruct((rows, cols), bf16),
        in_specs=[any_space],
        out_specs=any_space,
        scratch_shapes=[pltpu.SemaphoreType.DMA((chunks,))],
        compiler_params=pltpu.CompilerParams(vmem_limit_bytes=20 * 2**20),
        name="store",
    )(pltpu.with_memory_space_constraint(held, pltpu.VMEM))


def solution(mesh):
    return jax.shard_map(
        body,
        mesh=mesh,
        in_specs=(P("row", "col"), P(), P()),
        out_specs=P("row", "col"),
        check_vma=False,
    )
```

```python
import functools

import jax
import jax.numpy as jnp
from jax import lax
from jax.experimental import pallas as pl
from jax.experimental.pallas import tpu as pltpu
from jax.sharding import PartitionSpec as P

B = 64
P_SIZE = 256
LANES = 128
AHEAD = 1
MESH = pl.DeviceIdType.MESH
NT = (((1,), (1,)), ((), ()))


def nt_dot(a, b):
    return lax.dot_general(a, b, NT, preferred_element_type=jnp.float32)


def nn_dot(a, b):
    return jnp.dot(a, b, preferred_element_type=jnp.float32)


def one_hot(shape, test):
    i = lax.broadcasted_iota(jnp.int32, shape, 0)
    j = lax.broadcasted_iota(jnp.int32, shape, 1)
    return jnp.where(test(i, j), 1.0, 0.0).astype(jnp.bfloat16)


def gather_kernel(
    n_row, n_col,
    front, diag, fill, out,
    source, pan, colp, fac, colf, keep, w_lo, w_hi,
    load_sem, source_sem, row_recv, row_send, col_recv, col_send,
):
    r = lax.axis_index("row")
    c = lax.axis_index("col")
    rows, cols = out.shape
    heads = P_SIZE // B
    ratio = n_col // n_row
    half = 2 * ratio * B
    step_rows = 2 * half
    step_cols = step_rows // ratio
    chunks = rows // step_rows
    outer, inner = 4, n_col // 4
    a = c // inner
    b = c % inner
    owner = c < heads
    x, core = r // 2, r % 2
    source_row = c % n_row
    source_x, source_core = source_row // 2, source_row % 2
    parity = c // n_row
    n_x = n_row // 2

    def load(k):
        part = pl.ds(pl.multiple_of(k * step_rows, step_rows), step_rows)
        return pltpu.make_async_copy(front.at[part], out.at[part], load_sem.at[k])

    def fetch():
        return pltpu.make_async_copy(front.at[:, 0:LANES], source, source_sem)

    def row_copy(k, h, slot, target):
        return pltpu.make_async_remote_copy(
            src_ref=pan.at[k, h], dst_ref=pan.at[k, h],
            send_sem=row_send.at[k, h, slot], recv_sem=row_recv.at[k, h],
            device_id=(r, target), device_id_type=MESH,
        )

    def row_sends(k, h, act):
        a_h, b_h = h // inner, h % inner

        @pl.when(b == b_h)
        def _():
            @pl.when(jnp.logical_and(a >= a_h, a < outer - 1))
            def _():
                act(row_copy(k, h, 0, c + inner))

            @pl.when(jnp.logical_and(a <= a_h, a > 0))
            def _():
                act(row_copy(k, h, 1, c - inner))

            for d in range(1, inner):
                act(row_copy(k, h, 1 + d, a * inner + (b + d) % inner))

    def col_copy(k, src, slot, target):
        return pltpu.make_async_remote_copy(
            src_ref=src, dst_ref=colp.at[k],
            send_sem=col_send.at[k, slot], recv_sem=col_recv.at[k],
            device_id=(target, c), device_id_type=MESH,
        )

    def col_local(k):
        return pltpu.make_async_copy(pan.at[k, :, :, parity], colp.at[k], col_recv.at[k])

    is_source = r == source_row
    is_relay = jnp.logical_and(core == source_core, x != source_x)

    def col_source_sends(k, act):
        @pl.when(is_source)
        def _():
            src = pan.at[k, :, :, parity]
            for d in range(1, n_x):
                act(col_copy(k, src, d, ((x + d) % n_x) * 2 + core))
            act(col_copy(k, src, 0, x * 2 + 1 - core))

    def col_relay_sends(k, act):
        @pl.when(is_relay)
        def _():
            act(col_copy(k, colp.at[k], 0, x * 2 + 1 - core))

    @pl.when(owner)
    def _():
        fetch().start()

    for k in range(chunks):
        load(k).start()

    barrier = pltpu.get_barrier_semaphore()

    @pl.when(a > 0)
    def _():
        pl.semaphore_signal(barrier, inc=1, device_id=(r, c - inner), device_id_type=MESH)

    @pl.when(a < outer - 1)
    def _():
        pl.semaphore_signal(barrier, inc=1, device_id=(r, c + inner), device_id_type=MESH)

    for d in range(1, inner):
        pl.semaphore_signal(
            barrier, inc=1, device_id=(r, a * inner + (b + d) % inner), device_id_type=MESH
        )
    for d in range(1, n_row):
        pl.semaphore_signal(barrier, inc=1, device_id=((r + d) % n_row, c), device_id_type=MESH)

    @pl.when(owner)
    def _():
        fetch().wait()
        to_lo = one_hot((LANES, LANES), lambda i, j: (i == j) & (i < B))
        to_hi = one_hot((LANES, LANES), lambda i, j: (i + B == j) & (i < B))

        def pack(k, _):
            at = pl.multiple_of(k * step_rows, step_rows)
            both = nn_dot(source[pl.ds(at, half), :], to_lo)
            both += nn_dot(source[pl.ds(at + half, half), :], to_hi)
            pan[k, c] = both.astype(jnp.bfloat16).reshape(2, ratio, B, LANES)
            return 0

        lax.fori_loop(0, chunks, pack, 0)

    extra = jnp.where(a > 0, 1, 0) + jnp.where(a < outer - 1, 1, 0)
    pl.semaphore_wait(barrier, inner - 1 + n_row - 1 + extra)

    def own_sends(k, act):
        for h in range(heads):
            @pl.when(c == h)
            def _():
                row_sends(k, h, act)

    for k in range(min(AHEAD, chunks)):
        own_sends(k, lambda copy: copy.start())

    def spread(shift):
        return one_hot(
            (P_SIZE, heads * LANES),
            lambda i, j: (i == (j // LANES) * B + j % LANES - shift)
            & (j % LANES >= shift) & (j % LANES < shift + B),
        )

    w_lo[...] = nn_dot(diag[...], spread(0)).astype(jnp.bfloat16)
    w_hi[...] = nn_dot(diag[...], spread(B)).astype(jnp.bfloat16)

    count = fill.shape[0]
    local_rows = rows // B
    pick = one_hot((local_rows, count), lambda i, j: j == i * n_row + r)
    picked = nn_dot(pick, fill[...].astype(jnp.float32).astype(jnp.bfloat16)).astype(jnp.bfloat16)

    def make_keep(j, _):
        at = pl.multiple_of(j * step_cols, step_cols)
        widen = one_hot(
            (count, step_cols), lambda i, l: i == ((at + l) // B) * n_col + c
        )
        wide = nn_dot(picked, widen)
        i = lax.broadcasted_iota(jnp.int32, wide.shape, 0)
        l = lax.broadcasted_iota(jnp.int32, wide.shape, 1)
        live = (i * n_row + r >= heads) & (((at + l) // B) * n_col + c >= heads)
        keep[:, pl.ds(at, step_cols)] = jnp.where(live, wide, 0.0)
        return 0

    lax.fori_loop(0, cols // step_cols, make_keep, 0)

    step_blocks = step_rows // B
    to_front = one_hot((P_SIZE, LANES), lambda i, l: (i == c * B + l) & (l < B))

    def tile(i, j):
        row_at = pl.multiple_of(i * step_rows, step_rows)
        col_at = pl.multiple_of(j * step_cols, step_cols)
        part = (pl.ds(row_at, step_rows), pl.ds(col_at, step_cols))
        product = nt_dot(fac[part[0], :], colf[part[1], :])
        marks = keep[pl.ds(pl.multiple_of(i * step_blocks, step_blocks), step_blocks), part[1]]
        masked = product.reshape(step_blocks, B, step_cols) * marks[:, None, :]
        value = out[part].astype(jnp.float32) - masked.reshape(step_rows, step_cols)
        out[part] = value.astype(jnp.bfloat16)

    def arrive(k):
        @pl.when(k + AHEAD < chunks)
        def _():
            own_sends(k + AHEAD, lambda copy: copy.start())

        for h in range(heads):
            @pl.when(c != h)
            def _():
                row_copy(k, h, 0, c).wait_recv()
                row_sends(k, h, lambda copy: copy.start())

        col_source_sends(k, lambda copy: copy.start())

        @pl.when(is_source)
        def _():
            col_local(k).start()

    def factors(k):
        packed = jnp.concatenate(
            [pan[k, h].reshape(half, LANES) for h in range(heads)], axis=1
        )
        at = pl.multiple_of(k * step_rows, step_rows)
        fac[pl.ds(at, half), :] = nt_dot(packed, w_lo[...]).astype(jnp.bfloat16)
        fac[pl.ds(at + half, half), :] = nt_dot(packed, w_hi[...]).astype(jnp.bfloat16)

    def col_factors(k):
        @pl.when(is_source)
        def _():
            col_local(k).wait()

        @pl.when(jnp.logical_not(is_source))
        def _():
            col_copy(k, colp.at[k], 0, r).wait_recv()

        col_relay_sends(k, lambda copy: copy.start())
        packed = jnp.concatenate(
            [colp[k, h].reshape(2 * B, LANES) for h in range(heads)], axis=1
        )
        at = pl.multiple_of(k * step_cols, step_cols)
        colf[pl.ds(at, 2 * B), :] = nt_dot(packed, w_lo[...]).astype(jnp.bfloat16)
        colf[pl.ds(at + 2 * B, 2 * B), :] = nt_dot(packed, w_hi[...]).astype(jnp.bfloat16)

    def wave(k):
        lax.fori_loop(0, k + 1, lambda j, _: (tile(k, j), 0)[1], 0)
        lax.fori_loop(0, k, lambda i, _: (tile(i, k), 0)[1], 0)

        @pl.when(owner)
        def _():
            at = pl.ds(pl.multiple_of(k * step_rows, step_rows), step_rows)
            piece = nn_dot(fac[at, :], to_front)
            old = out[at, 0:LANES].astype(jnp.float32)
            lane = lax.broadcasted_iota(jnp.int32, old.shape, 1)
            out[at, 0:LANES] = jnp.where(lane < B, piece, old).astype(jnp.bfloat16)

    def step(k, _):
        @pl.when(k < chunks)
        def _():
            arrive(k)
            factors(k)

        @pl.when(k > 0)
        def _():
            col_factors(k - 1)
            load(k - 1).wait()
            wave(k - 1)

        return 0

    lax.fori_loop(0, chunks + 1, step, 0)

    def drain(k, _):
        for h in range(heads):
            row_sends(k, h, lambda copy: copy.wait_send())
        col_source_sends(k, lambda copy: copy.wait_send())
        col_relay_sends(k, lambda copy: copy.wait_send())
        return 0

    lax.fori_loop(0, chunks, drain, 0)


def store_kernel(value, out, sems):
    parts = sems.shape[0]
    size = value.shape[0] // parts
    copies = [
        pltpu.make_async_copy(
            value.at[pl.ds(i * size, size)], out.at[pl.ds(i * size, size)], sems.at[i]
        )
        for i in range(parts)
    ]
    for copy in copies:
        copy.start()
    for copy in copies:
        copy.wait()


def body(front, diag_inverse, fill_pattern):
    rows, cols = front.shape
    n_row = lax.axis_size("row")
    n_col = lax.axis_size("col")
    heads = P_SIZE // B
    ratio = n_col // n_row
    step_rows = 4 * ratio * B
    chunks = rows // step_rows
    inner = n_col // 4
    bf16 = jnp.bfloat16
    any_space = pl.BlockSpec(memory_space=pl.ANY)
    vmem = pl.BlockSpec(memory_space=pltpu.VMEM)
    held = pl.pallas_call(
        functools.partial(gather_kernel, n_row, n_col),
        out_shape=pltpu.VMEM((rows, cols), bf16),
        in_specs=[any_space, vmem, vmem],
        out_specs=vmem,
        scratch_shapes=[
            pltpu.VMEM((rows, LANES), bf16),
            pltpu.VMEM((chunks, heads, 2, ratio, B, LANES), bf16),
            pltpu.VMEM((chunks, heads, 2, B, LANES), bf16),
            pltpu.VMEM((rows, P_SIZE), bf16),
            pltpu.VMEM((cols, P_SIZE), bf16),
            pltpu.VMEM((rows // B, cols), jnp.float32),
            pltpu.VMEM((P_SIZE, heads * LANES), bf16),
            pltpu.VMEM((P_SIZE, heads * LANES), bf16),
            pltpu.SemaphoreType.DMA((chunks,)),
            pltpu.SemaphoreType.DMA,
            pltpu.SemaphoreType.DMA((chunks, heads)),
            pltpu.SemaphoreType.DMA((chunks, heads, inner + 1)),
            pltpu.SemaphoreType.DMA((chunks,)),
            pltpu.SemaphoreType.DMA((chunks, n_row // 2)),
        ],
        compiler_params=pltpu.CompilerParams(
            collective_id=0, has_side_effects=True, vmem_limit_bytes=20 * 2**20
        ),
        name="gather_update",
    )(front, diag_inverse, fill_pattern)
    return pl.pallas_call(
        store_kernel,
        out_shape=jax.ShapeDtypeStruct((rows, cols), bf16),
        in_specs=[any_space],
        out_specs=any_space,
        scratch_shapes=[pltpu.SemaphoreType.DMA((chunks,))],
        compiler_params=pltpu.CompilerParams(vmem_limit_bytes=20 * 2**20),
        name="store",
    )(pltpu.with_memory_space_constraint(held, pltpu.VMEM))


def solution(mesh):
    return jax.shard_map(
        body,
        mesh=mesh,
        in_specs=(P("row", "col"), P(), P()),
        out_specs=P("row", "col"),
        check_vma=False,
    )
```
